32 devices in a mesh: chan: 8 (over y, x, core), grp: 4 (over z).
Axes of the slice: x: 2, y: 2, z: 4, core: 2. Of those that a mesh axis runs over, the one named last changes fastest.
Arguments:
- raw_files: float32 [4, 2048, 1024], P('grp', 'chan'), may hold values from -6 to 6
- file_target: int32 [4, 2048], P('grp', 'chan'), may hold values from -1 to 511, as said below
- file_len: int32 [4, 2048], P('grp', 'chan'), may hold values from 768 to 1024
- fir_taps: float32 [64], replicated, may hold values from -0.75 to 0.75
- source_slot: int32 [8], replicated, may hold values from 0 to 15
Outputs:
- stacks: bfloat16 [8, 128, 256], P('grp', 'chan')
The draws below stay inside these ranges and needn't reach their ends.
Inputs may be any that keep to these rules, and one draw needn't show every extreme that they name: `file_target`: -1 marks an empty slot; any other entry o * 64 + j names file j of owner o, which holds channel o * 16 + j // 4, window (j // 2) % 2 and half j % 2 of that window. For each grp index every file of every owner stands in exactly one slot, so every owner receives exactly 64 files; a reader holds either none or exactly 32 files of one owner; some reader holds 256 files.
All inputs are finite; a program needn't handle non-finite values.
Results may differ from the reference program's by a relative error of at most 0.017.
Values may be sent and summed in bfloat16 or wider, within the bound.
A program may use at most 64 MiB of HBM per device.

```python
import math
import jax
import jax.numpy as jnp
from jax import lax

CB = 16
WINS = 2
WIN = 512
DEC = 4
TAPS = 64
LAGS = 256
ENVW = 64
RAWF = 1024
RECS = 64
CAP = 32
SLOTS = 256
VS = 8
N_CHAN = 8
N_GRP = 4


def draw_file_target(key, part):

    def one_group(group_key):
        key_order, key_random, key_local, key_slots = jax.random.split(group_key, 4)
        readers = N_CHAN
        pick_count = readers // 4
        source_order = jax.random.permutation(key_order, readers)
        favour = jnp.zeros((readers,), jnp.int32).at[source_order[:readers // 8]].set(1 << 20)
        favour = favour.at[source_order[0]].set(1 << 22)
        random_part = jax.random.randint(key_random, (readers, readers), 0, 1 << 20, dtype=jnp.int32)
        scores = (random_part + favour[None, :]) * readers + jnp.arange(readers, dtype=jnp.int32)[None, :]
        chosen = jnp.argsort(-scores, axis=1)[:, :pick_count].astype(jnp.int32)
        owner_rows = jnp.arange(readers, dtype=jnp.int32)[:, None]
        position = jnp.full((readers, readers), -1, jnp.int32).at[owner_rows, chosen].set(jnp.arange(pick_count, dtype=jnp.int32)[None, :])
        local_ids = jax.vmap(lambda one_key: jax.random.permutation(one_key, RECS))(jax.random.split(key_local, readers)).astype(jnp.int32)
        file_index = jnp.maximum(position, 0)[:, :, None] * CAP + jnp.arange(CAP, dtype=jnp.int32)[None, None, :]
        file_ids = local_ids[jnp.arange(readers, dtype=jnp.int32)[:, None, None], file_index] + owner_rows[:, :, None] * RECS
        file_ids = jnp.where(position[:, :, None] >= 0, file_ids, -1)
        by_reader = jnp.transpose(file_ids, (1, 0, 2)).reshape(readers, readers * CAP)
        shuffle = jax.vmap(lambda one_key: jax.random.permutation(one_key, readers * CAP))(jax.random.split(key_slots, readers)).astype(jnp.int32)
        return jnp.take_along_axis(by_reader, shuffle, axis=1).reshape(readers * readers * CAP)
    return jax.vmap(one_group)(jax.random.split(key, N_GRP))


def with_ends(values, own_key, low, high):
    extent = values.shape
    spot = [jax.random.randint(jax.random.fold_in(own_key, axis), (), 0, extent[axis]) for axis in range(len(extent))]
    values = values.at[tuple(spot)].set(low)
    longest = extent.index(max(extent))
    spot[longest] = (spot[longest] + 1) % extent[longest]
    return values.at[tuple(spot)].set(high)


def block_scale(stream_key, dims, cuts, least, top_value):
    level = 1.0
    for dim, parts in cuts:
        steps = jax.random.uniform(jax.random.fold_in(jax.random.fold_in(stream_key, 6), dim), (parts,), jnp.float32, least / len(cuts), top_value / len(cuts))
        level = level * jnp.repeat(jnp.exp(steps), dims[dim] // parts).reshape((-1,) + (1,) * (len(dims) - 1 - dim))
    return level


def noise(rng, dims, scale, reach, pieces=(), held_as=jnp.bfloat16):
    loudness = block_scale(rng, dims, pieces, -0.22, 0.18) if pieces else 1.0
    entries = jax.random.normal(rng, dims, jnp.float32) * scale * loudness
    return jnp.minimum(jnp.maximum(entries, -reach), reach).astype(held_as)


def setup_inputs(seed: int = 0) -> dict:
    seeds = jax.random.split(jax.random.key(seed), 6)
    return {
        "raw_files": noise(seeds[0], (N_GRP, N_CHAN * SLOTS, RAWF), 1.0, 6.0, ((0, 4), (1, 8)), jnp.float32),
        "file_target": draw_file_target(jax.random.fold_in(seeds[5], 71), 0),
        "file_len": with_ends(jax.random.randint(seeds[2], (N_GRP, N_CHAN * SLOTS), 3 * RAWF // 4, RAWF + 1), jax.random.fold_in(seeds[2], 1), 3 * RAWF // 4, RAWF).astype(jnp.int32),
        "fir_taps": noise(seeds[3], (TAPS,), TAPS ** -0.5, 0.75, (), jnp.float32),
        "source_slot": with_ends(jax.random.randint(seeds[4], (VS,), 0, CB), jax.random.fold_in(seeds[4], 1), 0, CB - 1).astype(jnp.int32),
    }


ENVELOPE_FLOOR = 0.3

def decimate(samples, lengths, fir_taps):
    sample_count = samples.shape[-1]
    trimmed = jnp.where(jnp.arange(sample_count, dtype=jnp.int32) < lengths[:, None], samples, jnp.zeros_like(samples))
    kernel = fir_taps[::-1].reshape(1, 1, TAPS)
    filtered = lax.conv_general_dilated(trimmed[:, None, :], kernel, (DEC,), [(TAPS - 1, 0)], precision=lax.Precision.HIGHEST)
    return filtered[:, 0, :]

def normalize(trace_rows):
    row_ids = jnp.arange(WIN, dtype=jnp.int32)[:, None]
    column_ids = jnp.arange(WIN, dtype=jnp.int32)[None, :]
    inside = (column_ids - row_ids >= -(ENVW // 2)) & (column_ids - row_ids < ENVW // 2)
    window_band = jnp.where(inside, 1.0 / ENVW, 0.0).astype(jnp.float32)
    envelope = jnp.dot(jnp.abs(trace_rows), window_band.T, precision=lax.Precision.HIGHEST)
    return (trace_rows / jnp.maximum(envelope, ENVELOPE_FLOOR)).astype(jnp.bfloat16)

def reference(raw_files, file_target, file_len, fir_taps, source_slot):
    lag_half = LAGS // 2
    period = WIN + lag_half
    span_len = WINS * period
    channel_total = CB * N_CHAN
    file_total = N_CHAN * RECS
    stack_scale = 1.0 / math.sqrt(N_GRP * WINS * WIN)
    source_channel = jnp.arange(N_CHAN, dtype=jnp.int32) * CB + source_slot
    receiver_list = []
    source_list = []
    for group_index in range(N_GRP):
        filtered = decimate(raw_files[group_index], file_len[group_index], fir_taps)
        targets = file_target[group_index]
        destination = jnp.where(targets < 0, file_total, targets)
        placed = jnp.zeros((file_total, RAWF // DEC), jnp.float32).at[destination].set(filtered, mode='drop')
        traces = normalize(placed.reshape(channel_total * WINS, WIN)).reshape(channel_total, WINS, WIN)
        widened = jnp.pad(traces.astype(jnp.float32), ((0, 0), (0, 0), (0, lag_half))).reshape(channel_total, span_len)
        receiver_list.append(widened)
        chosen = widened[source_channel]
        source_list.append(jnp.pad(chosen, ((0, 0), (lag_half, lag_half))))
    receivers = jnp.stack(receiver_list)
    sources = jnp.stack(source_list, axis=1)
    lag_index = jnp.arange(span_len, dtype=jnp.int32)[:, None] + jnp.arange(LAGS, dtype=jnp.int32)[None, :]
    channel_ids = jnp.arange(channel_total, dtype=jnp.int32)

    def one_source(inputs):
        source_rows, own_channel = inputs
        toeplitz = source_rows[:, lag_index]
        products = jnp.einsum('gcu,gul->gcl', receivers, toeplitz, precision=lax.Precision.HIGHEST)
        products = jnp.where((channel_ids == own_channel)[None, :, None], 0.0, products * stack_scale)
        rounded = lax.optimization_barrier(products.astype(jnp.bfloat16))
        return lax.optimization_barrier(jnp.sum(rounded.astype(jnp.float32), axis=0)).astype(jnp.bfloat16)
    return lax.map(one_source, (sources, source_channel))
```

```python
import functools
import math

import jax
import jax.numpy as jnp
from jax import lax
from jax.experimental import pallas as pl
from jax.experimental.pallas import tpu as pltpu
from jax.sharding import PartitionSpec as P

CB = 16
WINS = 2
WIN = 512
DEC = 4
TAPS = 64
LAGS = 256
ENVW = 64


ENVELOPE_FLOOR = 0.3
lag_step = 16


def shortened(array):
    return jax.tree.map(lambda a: a.astype(jnp.bfloat16) if a.dtype == jnp.float32 else a, array)


def decimate(samples, lengths, fir_taps):
    sample_count = samples.shape[-1]
    trimmed = jnp.where(
        jnp.arange(sample_count, dtype=jnp.int32) < lengths[:, None],
        samples,
        jnp.zeros_like(samples),
    )
    kernel = fir_taps[::-1].reshape(1, 1, TAPS)
    filtered = lax.conv_general_dilated(
        trimmed[:, None, :], kernel, (DEC,), [(TAPS - 1, 0)], precision=lax.Precision.HIGHEST
    )
    return filtered[:, 0, :]


def normalize(trace_rows):
    row_ids = jnp.arange(WIN, dtype=jnp.int32)[:, None]
    column_ids = jnp.arange(WIN, dtype=jnp.int32)[None, :]
    inside = (column_ids - row_ids >= -(ENVW // 2)) & (column_ids - row_ids < ENVW // 2)
    window_band = jnp.where(inside, 1.0 / ENVW, 0.0).astype(jnp.float32)
    envelope = jnp.dot(jnp.abs(trace_rows), window_band.T, precision=lax.Precision.HIGHEST)
    return (trace_rows / jnp.maximum(envelope, ENVELOPE_FLOOR)).astype(jnp.bfloat16)


def shifted_receivers(receivers):
    lag_half = LAGS // 2
    channel_count, window_count, _ = receivers.shape
    span_len = window_count * (WIN + lag_half)
    flattened = jnp.pad(receivers, ((0, 0), (0, 0), (0, lag_half))).reshape(channel_count, span_len)
    widened = jnp.pad(flattened, ((0, 0), (lag_step, 0)))
    copies = [
        lax.slice_in_dim(widened, lag_step - offset, lag_step - offset + span_len, 1, 1)
        for offset in range(lag_step)
    ]
    return jnp.stack(copies).reshape(lag_step * channel_count, span_len)


def correlate(shifted, sources, own_first, source_slot, stack_scale):
    lag_half = LAGS // 2
    row_count = sources.shape[0]
    channel_count = shifted.shape[0] // lag_step
    span_len = shifted.shape[1]
    window_count = span_len // (WIN + lag_half)
    padded = jnp.pad(sources.reshape(row_count, window_count, WIN), ((0, 0), (0, 0), (0, lag_half)))
    padded = jnp.pad(padded.reshape(row_count, span_len), ((0, 0), (lag_half, lag_half)))
    blocks = []
    for lag_block in range(LAGS // lag_step):
        window_view = lax.slice_in_dim(
            padded, lag_block * lag_step, lag_block * lag_step + span_len, 1, 1
        )
        blocks.append(
            lax.dot_general(
                window_view, shifted, (((1,), (1,)), ((), ())), preferred_element_type=jnp.float32
            )
        )
    result = jnp.stack(blocks, axis=1).reshape(row_count, LAGS // lag_step, lag_step, channel_count)
    result = jnp.transpose(result, (0, 3, 1, 2)).reshape(row_count, channel_count, LAGS)
    owners = jnp.arange(row_count, dtype=jnp.int32)
    source_channel = owners * CB + source_slot
    receiver_channel = own_first + jnp.arange(channel_count, dtype=jnp.int32)
    distinct = source_channel[:, None] != receiver_channel[None, :]
    return jnp.where(distinct[:, :, None], result * stack_scale, 0.0)


def local(raw_files, file_target, file_len, fir_taps, source_slot):
    owner_count = lax.axis_size("chan")
    group_count = lax.axis_size("grp")
    slot_count = raw_files.shape[1]
    capacity = slot_count // owner_count
    file_count = 2 * CB * WINS
    targets = file_target[0]
    owner_of = jnp.where(targets >= 0, targets // file_count, -1)
    local_id = jnp.where(targets >= 0, targets % file_count, -1)
    positions = jnp.arange(slot_count, dtype=jnp.int32)
    earlier = (owner_of[None, :] == owner_of[:, None]) & (positions[None, :] < positions[:, None])
    slot_rank = jnp.sum(earlier.astype(jnp.int32), axis=1)
    slot_index = jnp.where(targets >= 0, owner_of * capacity + slot_rank, slot_count)

    def pack_slots(values, fill_value):
        buffer = (
            jnp.full((slot_count,) + values.shape[1:], fill_value, values.dtype)
            .at[slot_index]
            .set(values, mode="drop")
        )
        return buffer.reshape((owner_count, capacity) + values.shape[1:])

    ids_packed = pack_slots(local_id, -1)
    filtered = decimate(raw_files[0], file_len[0], fir_taps)
    received, received_ids = (
        lax.all_to_all(
            shortened(pack_slots(filtered, 0.0)), "chan", split_axis=0, concat_axis=0, tiled=True
        ),
        lax.all_to_all(ids_packed, "chan", split_axis=0, concat_axis=0, tiled=True),
    )
    half_len = received.shape[-1]
    destination = received_ids.reshape(-1)
    destination = jnp.where(destination < 0, file_count, destination)
    placed = (
        jnp.zeros((file_count, half_len), jnp.float32)
        .at[destination]
        .set(received.reshape(-1, half_len), mode="drop")
    )
    traces = normalize(placed.reshape(CB * WINS, WIN)).reshape(CB, WINS, WIN)
    stack_scale = 1.0 / math.sqrt(group_count * WINS * WIN)
    chan_index = lax.axis_index("chan")
    own_slot = lax.dynamic_slice_in_dim(source_slot, chan_index, 1)[0]
    own_source = lax.dynamic_slice_in_dim(traces, own_slot, 1, 0).reshape(1, WINS * WIN)
    own_first = chan_index * CB
    shifted = shifted_receivers(traces)
    term_rows = correlate(
        shifted,
        lax.all_gather(own_source, "chan", axis=0, tiled=True),
        own_first,
        source_slot,
        stack_scale,
    )
    stacks = lax.psum_scatter(
        term_rows.astype(jnp.bfloat16), "grp", scatter_dimension=0, tiled=True
    )
    return stacks


def iota(shape, dim):
    return lax.broadcasted_iota(jnp.int32, shape, dim)


def column_of(row):
    count = row.shape[1]
    square = (count, count)
    return jnp.sum(jnp.where(iota(square, 0) == iota(square, 1), row, 0.0), axis=1, keepdims=True)


def fir_matrix(taps_row):
    taps_column = column_of(taps_row)
    spread = (TAPS, 128)
    reverse = jnp.sum(
        jnp.where(iota(spread, 0) + iota(spread, 1) == TAPS - 1, taps_column, 0.0), axis=0, keepdims=True
    )
    raw_len = 1024
    half_len = raw_len // DEC
    wide = jnp.concatenate([reverse, jnp.zeros((1, raw_len - 128), jnp.float32)], axis=1)
    wide = jnp.broadcast_to(wide, (8, raw_len))
    block = pltpu.roll(wide, raw_len - TAPS + 1, 1, stride=DEC, stride_axis=0)
    rows = [block if i == 0 else pltpu.roll(block, 8 * DEC * i, 1) for i in range(half_len // 8)]
    matrix = jnp.concatenate(rows, axis=0)
    return jnp.where(iota(matrix.shape, 1) <= DEC * iota(matrix.shape, 0), matrix, 0.0)


def split(values):
    high = values.astype(jnp.bfloat16)
    return high, (values - high.astype(jnp.float32)).astype(jnp.bfloat16)


def dot_rows(a, b):
    return lax.dot_general(a, b, (((1,), (1,)), ((), ())), preferred_element_type=jnp.float32)


def dot(a, b):
    return jnp.dot(a, b, preferred_element_type=jnp.float32)


def kernel(
    owner_count, group_count, stack_scale,
    raw_ref, target_ref, len_ref, taps_ref, slot_ref, out_ref,
    files, arrived, own_source, sources, terms, sums, band_ref, flip_ref,
    file_send, file_recv, source_send, source_recv, sum_send, sum_recv,
):
    me = lax.axis_index("chan")
    group = lax.axis_index("grp")
    slot_count = raw_ref.shape[1]
    file_count = 2 * CB * WINS
    per_group = owner_count // group_count
    lag_half = LAGS // 2

    barrier = pltpu.get_barrier_semaphore()
    for step in range(1, owner_count):
        pl.semaphore_signal(
            barrier, inc=1, device_id={"chan": lax.rem(me + step, owner_count)}, device_id_type=pl.DeviceIdType.MESH
        )
    for step in range(1, group_count):
        pl.semaphore_signal(
            barrier, inc=1, device_id={"grp": lax.rem(group + step, group_count)}, device_id_type=pl.DeviceIdType.MESH
        )

    lengths = column_of(len_ref[...].astype(jnp.float32)).astype(jnp.int32)
    raw = raw_ref[0]
    trimmed = jnp.where(iota(raw.shape, 1) < lengths, raw, 0.0)
    raw_high, raw_low = split(trimmed)
    fir_high, fir_low = split(fir_matrix(taps_ref[...]))
    filtered = dot_rows(raw_high, fir_high) + (dot_rows(raw_low, fir_high) + dot_rows(raw_high, fir_low))
    filtered = filtered.astype(jnp.bfloat16)

    shape = (owner_count * file_count, slot_count)
    place = iota(shape, 0)
    within = place % file_count
    wanted = (
        place - within
        + 2 * (2 * (within % CB) + (within // CB) % WINS)
        + within // (CB * WINS)
    )
    pick = jnp.where(wanted == target_ref[...], 1.0, 0.0).astype(jnp.bfloat16)
    files[...] = dot(pick, filtered).astype(jnp.bfloat16).reshape(files.shape)

    pl.semaphore_wait(barrier, owner_count + group_count - 2)

    def to_owner(step, source, landing, send, recv):
        return pltpu.make_async_remote_copy(
            src_ref=source, dst_ref=landing, send_sem=send.at[step - 1], recv_sem=recv.at[step - 1],
            device_id={"chan": lax.rem(me + step, owner_count)}, device_id_type=pl.DeviceIdType.MESH,
        )

    file_copies = [
        to_owner(step, files.at[lax.rem(me + step, owner_count)], arrived.at[step - 1], file_send, file_recv)
        for step in range(1, owner_count)
    ]
    for copy in file_copies:
        copy.start()
    square = (WIN, WIN)
    ahead = iota(square, 0) - iota(square, 1)
    inside = (ahead >= -(ENVW // 2)) & (ahead < ENVW // 2)
    band_ref[...] = jnp.where(inside, 1.0 / ENVW, 0.0).astype(jnp.bfloat16)
    mirrored = iota(square, 0) + iota(square, 1) == WIN - 1
    flip_ref[...] = jnp.where(mirrored, 1.0, 0.0).astype(jnp.bfloat16)
    placed = files[me].astype(jnp.float32)
    for step, copy in enumerate(file_copies):
        copy.wait_recv()
        placed = placed + arrived[step].astype(jnp.float32)

    rows = CB * WINS
    trace = jnp.concatenate([placed[:rows], placed[rows:]], axis=1)
    envelope = dot(jnp.abs(trace).astype(jnp.bfloat16), band_ref[...])
    normal = trace / jnp.maximum(envelope, ENVELOPE_FLOOR)
    chosen = iota((CB, 1), 0) == slot_ref[me]
    own = jnp.concatenate(
        [
            jnp.sum(jnp.where(chosen, normal[w * CB:(w + 1) * CB], 0.0), axis=0, keepdims=True)
            for w in range(WINS)
        ],
        axis=1,
    )
    own_source[...] = own
    sources[me] = own
    source_copies = [
        to_owner(step, own_source, sources.at[me], source_send, source_recv) for step in range(1, owner_count)
    ]
    for copy in source_copies:
        copy.start()
    flipped = dot(normal.astype(jnp.bfloat16), flip_ref[...]).astype(jnp.bfloat16)
    receivers = jnp.concatenate([flipped[w * CB:(w + 1) * CB] for w in range(WINS)], axis=1)
    for copy in source_copies:
        copy.wait_recv()

    def correlation(owner):
        source = sources[owner].astype(jnp.bfloat16).astype(jnp.float32)
        pieces = []
        for w in range(WINS):
            row = jnp.concatenate(
                [source[:, w * WIN:(w + 1) * WIN], jnp.zeros((1, LAGS), jnp.float32)], axis=1
            )
            row = jnp.broadcast_to(row, (lag_half, WIN + LAGS))
            shifted = pltpu.roll(row, 1, 1, stride=1, stride_axis=0).astype(jnp.bfloat16)
            for begin in range(WIN - 128, -1, -128):
                pieces.append(shifted[:, begin:begin + LAGS])
        result = dot(receivers, jnp.concatenate(pieces, axis=0)) * stack_scale
        own_row = iota((CB, 1), 0) + me * CB == owner * CB + slot_ref[owner]
        return jnp.where(own_row, 0.0, result).astype(jnp.bfloat16)

    sum_copies = []
    for step in list(range(1, group_count)) + [0]:
        peer = lax.rem(group + step, group_count)
        for index in range(per_group):
            terms[step, index] = correlation(peer * per_group + index)
        if step:
            copy = pltpu.make_async_remote_copy(
                src_ref=terms.at[step], dst_ref=sums.at[step - 1],
                send_sem=sum_send.at[step - 1], recv_sem=sum_recv.at[step - 1],
                device_id={"grp": peer}, device_id_type=pl.DeviceIdType.MESH,
            )
            copy.start()
            sum_copies.append(copy)
    total = terms[0].astype(jnp.float32)
    for step, copy in enumerate(sum_copies):
        copy.wait_recv()
        total = total + sums[step].astype(jnp.float32)
    out_ref[...] = total.astype(jnp.bfloat16)
    for copy in file_copies + source_copies + sum_copies:
        copy.wait_send()


def fused(raw_files, file_target, file_len, fir_taps, source_slot):
    owner_count = lax.axis_size("chan")
    group_count = lax.axis_size("grp")
    file_count = 2 * CB * WINS
    half_len = raw_files.shape[2] // DEC
    per_group = owner_count // group_count
    stack_scale = 1.0 / math.sqrt(group_count * WINS * WIN)
    vmem = pl.BlockSpec(memory_space=pltpu.VMEM)
    dma = pltpu.SemaphoreType.DMA
    return pl.pallas_call(
        functools.partial(kernel, owner_count, group_count, stack_scale),
        out_shape=jax.ShapeDtypeStruct((per_group, CB, LAGS), jnp.bfloat16),
        in_specs=[vmem] * 4 + [pl.BlockSpec(memory_space=pltpu.SMEM)],
        out_specs=vmem,
        scratch_shapes=[
            pltpu.VMEM((owner_count, file_count, half_len), jnp.bfloat16),
            pltpu.VMEM((owner_count - 1, file_count, half_len), jnp.bfloat16),
            pltpu.VMEM((1, WINS * WIN), jnp.float32),
            pltpu.VMEM((owner_count, 1, WINS * WIN), jnp.float32),
            pltpu.VMEM((group_count, per_group, CB, LAGS), jnp.bfloat16),
            pltpu.VMEM((group_count - 1, per_group, CB, LAGS), jnp.bfloat16),
            pltpu.VMEM((WIN, WIN), jnp.bfloat16),
            pltpu.VMEM((WIN, WIN), jnp.bfloat16),
            dma((owner_count - 1,)), dma((owner_count - 1,)),
            dma((owner_count - 1,)), dma((owner_count - 1,)),
            dma((group_count - 1,)), dma((group_count - 1,)),
        ],
        compiler_params=pltpu.CompilerParams(
            collective_id=0, has_side_effects=True, vmem_limit_bytes=48 * 1024 * 1024
        ),
    )(raw_files, file_target, file_len, fir_taps.reshape(1, TAPS), source_slot)


def solution(mesh):
    placed = (P("grp", "chan", None), P("grp", "chan"), P("grp", "chan"), P(), P())
    body = fused if mesh.shape["chan"] <= 16 else local
    return jax.shard_map(
        body, mesh=mesh, in_specs=placed, out_specs=P("grp", "chan", None), check_vma=False
    )
```

```python
import functools
import math

import jax
import jax.numpy as jnp
from jax import lax
from jax.experimental import pallas as pl
from jax.experimental.pallas import tpu as pltpu
from jax.sharding import PartitionSpec as P

CB = 16
WINS = 2
WIN = 512
DEC = 4
TAPS = 64
LAGS = 256
ENVW = 64


ENVELOPE_FLOOR = 0.3
lag_step = 16


def shortened(array):
    return jax.tree.map(lambda a: a.astype(jnp.bfloat16) if a.dtype == jnp.float32 else a, array)


def decimate(samples, lengths, fir_taps):
    sample_count = samples.shape[-1]
    trimmed = jnp.where(
        jnp.arange(sample_count, dtype=jnp.int32) < lengths[:, None],
        samples,
        jnp.zeros_like(samples),
    )
    kernel = fir_taps[::-1].reshape(1, 1, TAPS)
    filtered = lax.conv_general_dilated(
        trimmed[:, None, :], kernel, (DEC,), [(TAPS - 1, 0)], precision=lax.Precision.HIGHEST
    )
    return filtered[:, 0, :]


def normalize(trace_rows):
    row_ids = jnp.arange(WIN, dtype=jnp.int32)[:, None]
    column_ids = jnp.arange(WIN, dtype=jnp.int32)[None, :]
    inside = (column_ids - row_ids >= -(ENVW // 2)) & (column_ids - row_ids < ENVW // 2)
    window_band = jnp.where(inside, 1.0 / ENVW, 0.0).astype(jnp.float32)
    envelope = jnp.dot(jnp.abs(trace_rows), window_band.T, precision=lax.Precision.HIGHEST)
    return (trace_rows / jnp.maximum(envelope, ENVELOPE_FLOOR)).astype(jnp.bfloat16)


def shifted_receivers(receivers):
    lag_half = LAGS // 2
    channel_count, window_count, _ = receivers.shape
    span_len = window_count * (WIN + lag_half)
    flattened = jnp.pad(receivers, ((0, 0), (0, 0), (0, lag_half))).reshape(channel_count, span_len)
    widened = jnp.pad(flattened, ((0, 0), (lag_step, 0)))
    copies = [
        lax.slice_in_dim(widened, lag_step - offset, lag_step - offset + span_len, 1, 1)
        for offset in range(lag_step)
    ]
    return jnp.stack(copies).reshape(lag_step * channel_count, span_len)


def correlate(shifted, sources, own_first, source_slot, stack_scale):
    lag_half = LAGS // 2
    row_count = sources.shape[0]
    channel_count = shifted.shape[0] // lag_step
    span_len = shifted.shape[1]
    window_count = span_len // (WIN + lag_half)
    padded = jnp.pad(sources.reshape(row_count, window_count, WIN), ((0, 0), (0, 0), (0, lag_half)))
    padded = jnp.pad(padded.reshape(row_count, span_len), ((0, 0), (lag_half, lag_half)))
    blocks = []
    for lag_block in range(LAGS // lag_step):
        window_view = lax.slice_in_dim(
            padded, lag_block * lag_step, lag_block * lag_step + span_len, 1, 1
        )
        blocks.append(
            lax.dot_general(
                window_view, shifted, (((1,), (1,)), ((), ())), preferred_element_type=jnp.float32
            )
        )
    result = jnp.stack(blocks, axis=1).reshape(row_count, LAGS // lag_step, lag_step, channel_count)
    result = jnp.transpose(result, (0, 3, 1, 2)).reshape(row_count, channel_count, LAGS)
    owners = jnp.arange(row_count, dtype=jnp.int32)
    source_channel = owners * CB + source_slot
    receiver_channel = own_first + jnp.arange(channel_count, dtype=jnp.int32)
    distinct = source_channel[:, None] != receiver_channel[None, :]
    return jnp.where(distinct[:, :, None], result * stack_scale, 0.0)


def local(raw_files, file_target, file_len, fir_taps, source_slot):
    owner_count = lax.axis_size("chan")
    group_count = lax.axis_size("grp")
    slot_count = raw_files.shape[1]
    capacity = slot_count // owner_count
    file_count = 2 * CB * WINS
    targets = file_target[0]
    owner_of = jnp.where(targets >= 0, targets // file_count, -1)
    local_id = jnp.where(targets >= 0, targets % file_count, -1)
    positions = jnp.arange(slot_count, dtype=jnp.int32)
    earlier = (owner_of[None, :] == owner_of[:, None]) & (positions[None, :] < positions[:, None])
    slot_rank = jnp.sum(earlier.astype(jnp.int32), axis=1)
    slot_index = jnp.where(targets >= 0, owner_of * capacity + slot_rank, slot_count)

    def pack_slots(values, fill_value):
        buffer = (
            jnp.full((slot_count,) + values.shape[1:], fill_value, values.dtype)
            .at[slot_index]
            .set(values, mode="drop")
        )
        return buffer.reshape((owner_count, capacity) + values.shape[1:])

    ids_packed = pack_slots(local_id, -1)
    filtered = decimate(raw_files[0], file_len[0], fir_taps)
    received, received_ids = (
        lax.all_to_all(
            shortened(pack_slots(filtered, 0.0)), "chan", split_axis=0, concat_axis=0, tiled=True
        ),
        lax.all_to_all(ids_packed, "chan", split_axis=0, concat_axis=0, tiled=True),
    )
    half_len = received.shape[-1]
    destination = received_ids.reshape(-1)
    destination = jnp.where(destination < 0, file_count, destination)
    placed = (
        jnp.zeros((file_count, half_len), jnp.float32)
        .at[destination]
        .set(received.reshape(-1, half_len), mode="drop")
    )
    traces = normalize(placed.reshape(CB * WINS, WIN)).reshape(CB, WINS, WIN)
    stack_scale = 1.0 / math.sqrt(group_count * WINS * WIN)
    chan_index = lax.axis_index("chan")
    own_slot = lax.dynamic_slice_in_dim(source_slot, chan_index, 1)[0]
    own_source = lax.dynamic_slice_in_dim(traces, own_slot, 1, 0).reshape(1, WINS * WIN)
    own_first = chan_index * CB
    shifted = shifted_receivers(traces)
    term_rows = correlate(
        shifted,
        lax.all_gather(own_source, "chan", axis=0, tiled=True),
        own_first,
        source_slot,
        stack_scale,
    )
    stacks = lax.psum_scatter(
        term_rows.astype(jnp.bfloat16), "grp", scatter_dimension=0, tiled=True
    )
    return stacks


def iota(shape, dim):
    return lax.broadcasted_iota(jnp.int32, shape, dim)


def column_of(row):
    count = row.shape[1]
    square = (count, count)
    return jnp.sum(jnp.where(iota(square, 0) == iota(square, 1), row, 0.0), axis=1, keepdims=True)


def fir_matrix(taps_row):
    taps_column = column_of(taps_row)
    spread = (TAPS, 128)
    reverse = jnp.sum(
        jnp.where(iota(spread, 0) + iota(spread, 1) == TAPS - 1, taps_column, 0.0), axis=0, keepdims=True
    )
    raw_len = 1024
    half_len = raw_len // DEC
    wide = jnp.concatenate([reverse, jnp.zeros((1, raw_len - 128), jnp.float32)], axis=1)
    wide = jnp.broadcast_to(wide, (8, raw_len))
    block = pltpu.roll(wide, raw_len - TAPS + 1, 1, stride=DEC, stride_axis=0)
    rows = [block if i == 0 else pltpu.roll(block, 8 * DEC * i, 1) for i in range(half_len // 8)]
    matrix = jnp.concatenate(rows, axis=0)
    return jnp.where(iota(matrix.shape, 1) <= DEC * iota(matrix.shape, 0), matrix, 0.0)


def split(values):
    high = values.astype(jnp.bfloat16)
    return high, (values - high.astype(jnp.float32)).astype(jnp.bfloat16)


def dot_rows(a, b):
    return lax.dot_general(a, b, (((1,), (1,)), ((), ())), preferred_element_type=jnp.float32)


def dot(a, b):
    return jnp.dot(a, b, preferred_element_type=jnp.float32)


def kernel(
    owner_count, group_count, stack_scale,
    raw_in, target_in, len_in, taps_in, slot_in, out_ref,
    raw_ref, target_ref, len_ref, taps_ref, slot_ref, load_sem,
    files, arrived, own_source, sources, terms, sums, band_ref, flip_ref,
    file_send, file_recv, source_send, source_recv, sum_send, sum_recv,
):
    me = lax.axis_index("chan")
    group = lax.axis_index("grp")
    slot_count = raw_ref.shape[1]
    file_count = 2 * CB * WINS
    per_group = owner_count // group_count
    lag_half = LAGS // 2

    loads = [
        pltpu.make_async_copy(source, landing, load_sem.at[index])
        for index, (source, landing) in enumerate((
            (taps_in, taps_ref), (len_in, len_ref), (raw_in, raw_ref), (target_in, target_ref), (slot_in, slot_ref),
        ))
    ]
    for load in loads:
        load.start()
    barrier = pltpu.get_barrier_semaphore()
    for step in range(1, owner_count):
        pl.semaphore_signal(
            barrier, inc=1, device_id={"chan": lax.rem(me + step, owner_count)}, device_id_type=pl.DeviceIdType.MESH
        )
    for step in range(1, group_count):
        pl.semaphore_signal(
            barrier, inc=1, device_id={"grp": lax.rem(group + step, group_count)}, device_id_type=pl.DeviceIdType.MESH
        )

    loads[0].wait()
    fir_high, fir_low = split(fir_matrix(taps_ref[...]))
    for load in loads[1:]:
        load.wait()
    lengths = column_of(len_ref[...].astype(jnp.float32)).astype(jnp.int32)
    raw = raw_ref[0]
    trimmed = jnp.where(iota(raw.shape, 1) < lengths, raw, 0.0)
    raw_high, raw_low = split(trimmed)
    filtered = dot_rows(raw_high, fir_high) + (dot_rows(raw_low, fir_high) + dot_rows(raw_high, fir_low))
    filtered = filtered.astype(jnp.bfloat16)

    shape = (owner_count * file_count, slot_count)
    place = iota(shape, 0)
    within = place % file_count
    wanted = (
        place - within
        + 2 * (2 * (within % CB) + (within // CB) % WINS)
        + within // (CB * WINS)
    )
    pick = jnp.where(wanted == target_ref[...], 1.0, 0.0).astype(jnp.bfloat16)
    files[...] = dot(pick, filtered).astype(jnp.bfloat16).reshape(files.shape)

    pl.semaphore_wait(barrier, owner_count + group_count - 2)

    def to_owner(step, source, landing, send, recv):
        return pltpu.make_async_remote_copy(
            src_ref=source, dst_ref=landing, send_sem=send.at[step - 1], recv_sem=recv.at[step - 1],
            device_id={"chan": lax.rem(me + step, owner_count)}, device_id_type=pl.DeviceIdType.MESH,
        )

    file_copies = [
        to_owner(step, files.at[lax.rem(me + step, owner_count)], arrived.at[step - 1], file_send, file_recv)
        for step in range(1, owner_count)
    ]
    for copy in file_copies:
        copy.start()
    square = (WIN, WIN)
    ahead = iota(square, 0) - iota(square, 1)
    inside = (ahead >= -(ENVW // 2)) & (ahead < ENVW // 2)
    band_ref[...] = jnp.where(inside, 1.0 / ENVW, 0.0).astype(jnp.bfloat16)
    mirrored = iota(square, 0) + iota(square, 1) == WIN - 1
    flip_ref[...] = jnp.where(mirrored, 1.0, 0.0).astype(jnp.bfloat16)
    placed = files[me].astype(jnp.float32)
    for step, copy in enumerate(file_copies):
        copy.wait_recv()
        placed = placed + arrived[step].astype(jnp.float32)

    rows = CB * WINS
    trace = jnp.concatenate([placed[:rows], placed[rows:]], axis=1)
    envelope = dot(jnp.abs(trace).astype(jnp.bfloat16), band_ref[...])
    normal = trace / jnp.maximum(envelope, ENVELOPE_FLOOR)
    chosen = iota((CB, 1), 0) == slot_ref[me]
    own = jnp.concatenate(
        [
            jnp.sum(jnp.where(chosen, normal[w * CB:(w + 1) * CB], 0.0), axis=0, keepdims=True)
            for w in range(WINS)
        ],
        axis=1,
    )
    own_source[...] = own
    sources[me] = own
    source_copies = [
        to_owner(step, own_source, sources.at[me], source_send, source_recv) for step in range(1, owner_count)
    ]
    for copy in source_copies:
        copy.start()
    flipped = dot(normal.astype(jnp.bfloat16), flip_ref[...]).astype(jnp.bfloat16)
    receivers = jnp.concatenate([flipped[w * CB:(w + 1) * CB] for w in range(WINS)], axis=1)
    for copy in source_copies:
        copy.wait_recv()

    def correlation(owner):
        source = sources[owner].astype(jnp.bfloat16).astype(jnp.float32)
        pieces = []
        for w in range(WINS):
            row = jnp.concatenate(
                [source[:, w * WIN:(w + 1) * WIN], jnp.zeros((1, LAGS), jnp.float32)], axis=1
            )
            row = jnp.broadcast_to(row, (lag_half, WIN + LAGS))
            shifted = pltpu.roll(row, 1, 1, stride=1, stride_axis=0).astype(jnp.bfloat16)
            for begin in range(WIN - 128, -1, -128):
                pieces.append(shifted[:, begin:begin + LAGS])
        result = dot(receivers, jnp.concatenate(pieces, axis=0)) * stack_scale
        own_row = iota((CB, 1), 0) + me * CB == owner * CB + slot_ref[owner]
        return jnp.where(own_row, 0.0, result).astype(jnp.bfloat16)

    sum_copies = []
    for step in list(range(1, group_count)) + [0]:
        peer = lax.rem(group + step, group_count)
        for index in range(per_group):
            terms[step, index] = correlation(peer * per_group + index)
        if step:
            copy = pltpu.make_async_remote_copy(
                src_ref=terms.at[step], dst_ref=sums.at[step - 1],
                send_sem=sum_send.at[step - 1], recv_sem=sum_recv.at[step - 1],
                device_id={"grp": peer}, device_id_type=pl.DeviceIdType.MESH,
            )
            copy.start()
            sum_copies.append(copy)
    total = terms[0].astype(jnp.float32)
    for step, copy in enumerate(sum_copies):
        copy.wait_recv()
        total = total + sums[step].astype(jnp.float32)
    out_ref[...] = total.astype(jnp.bfloat16)
    for copy in file_copies + source_copies + sum_copies:
        copy.wait_send()


def fused(raw_files, file_target, file_len, fir_taps, source_slot):
    owner_count = lax.axis_size("chan")
    group_count = lax.axis_size("grp")
    file_count = 2 * CB * WINS
    half_len = raw_files.shape[2] // DEC
    per_group = owner_count // group_count
    stack_scale = 1.0 / math.sqrt(group_count * WINS * WIN)
    vmem = pl.BlockSpec(memory_space=pltpu.VMEM)
    dma = pltpu.SemaphoreType.DMA
    return pl.pallas_call(
        functools.partial(kernel, owner_count, group_count, stack_scale),
        out_shape=jax.ShapeDtypeStruct((per_group, CB, LAGS), jnp.bfloat16),
        in_specs=[pl.BlockSpec(memory_space=pl.ANY)] * 5,
        out_specs=vmem,
        scratch_shapes=[
            pltpu.VMEM(raw_files.shape, raw_files.dtype),
            pltpu.VMEM(file_target.shape, file_target.dtype),
            pltpu.VMEM(file_len.shape, file_len.dtype),
            pltpu.VMEM((1, TAPS), fir_taps.dtype),
            pltpu.SMEM(source_slot.shape, source_slot.dtype),
            dma((5,)),
            pltpu.VMEM((owner_count, file_count, half_len), jnp.bfloat16),
            pltpu.VMEM((owner_count - 1, file_count, half_len), jnp.bfloat16),
            pltpu.VMEM((1, WINS * WIN), jnp.float32),
            pltpu.VMEM((owner_count, 1, WINS * WIN), jnp.float32),
            pltpu.VMEM((group_count, per_group, CB, LAGS), jnp.bfloat16),
            pltpu.VMEM((group_count - 1, per_group, CB, LAGS), jnp.bfloat16),
            pltpu.VMEM((WIN, WIN), jnp.bfloat16),
            pltpu.VMEM((WIN, WIN), jnp.bfloat16),
            dma((owner_count - 1,)), dma((owner_count - 1,)),
            dma((owner_count - 1,)), dma((owner_count - 1,)),
            dma((group_count - 1,)), dma((group_count - 1,)),
        ],
        compiler_params=pltpu.CompilerParams(
            collective_id=0, has_side_effects=True
        ),
    )(raw_files, file_target, file_len, fir_taps.reshape(1, TAPS), source_slot)


def solution(mesh):
    placed = (P("grp", "chan", None), P("grp", "chan"), P("grp", "chan"), P(), P())
    body = fused if mesh.shape["chan"] <= 16 else local
    return jax.shard_map(
        body, mesh=mesh, in_specs=placed, out_specs=P("grp", "chan", None), check_vma=False
    )
```
